32 devices in a mesh: dp: 8 (over y, x, core), tensor: 4 (over z).
Axes of the slice: x: 2, y: 2, z: 4, core: 2. Of those that a mesh axis runs over, the one named last changes fastest.
Arguments:
- hidden_in: bfloat16 [16, 1024, 768], P('dp', 'tensor'), may hold values from -6 to 6
- cotangent: bfloat16 [16, 1024, 768], P('dp', 'tensor'), may hold values from -6 to 6
- segment_ids: int32 [16, 1024], P('dp'), may hold values from 0 to 6, as said below
- w_qkv: bfloat16 [3, 768, 768], P(None, 'dp', 'tensor'), may hold values from -0.21875 to 0.21875
- w_out: bfloat16 [768, 768], P('tensor', 'dp'), may hold values from -1.25 to 1.25
- w_in: bfloat16 [2, 768, 1152], P(None, 'dp', 'tensor'), may hold values from -0.21875 to 0.21875
- w_down: bfloat16 [1152, 768], P('tensor', 'dp'), may hold values from -0.1875 to 0.1875
- norm_gains: bfloat16 [2, 768], P(None, 'dp'), may hold values from 0.099609375 to 1.8984375
Outputs:
- layer_out: bfloat16 [16, 1024, 768], P('dp', 'tensor')
- grad_input: bfloat16 [16, 1024, 768], P('dp', 'tensor')
- grad_qkv: float32 [3, 768, 768], P(None, 'dp', 'tensor')
- grad_out: float32 [768, 768], P('tensor', 'dp')
- grad_in: float32 [2, 768, 1152], P(None, 'dp', 'tensor')
- grad_down: float32 [1152, 768], P('tensor', 'dp')
- grad_gains: float32 [2, 768], P(None, 'dp')
The draws below stay inside these ranges and needn't reach their ends.
Inputs may be any that keep to these rules, and one draw needn't show every extreme that they name: `segment_ids`: each row starts with id 0 and its ids never fall, rising by one at each new document; documents are 204 to 2048 tokens long before they are cut at row ends, so only a row's first and last run may be shorter.
All inputs are finite; a program needn't handle non-finite values.
Results may differ from the reference program's by a relative error of at most 0.023.
Values may be sent and summed in bfloat16 or wider, within the bound.
A program may use at most 128 MiB of HBM per device.

```python
import math
import jax
import jax.numpy as jnp
from jax import lax

D = 768
H = 12
HD = 64
FF = 1152
L = 1024
ROWS = 16


def draw_segment_ids(key, part):
    shortest = max(L // 5, 1)
    doc_lengths = jax.random.randint(key, (ROWS, 16), shortest, 2 * L + 1)
    offset = jax.random.randint(jax.random.fold_in(key, 7), (ROWS, 1), 0, doc_lengths[:, :1])
    row_index = jnp.arange(ROWS, dtype=jnp.int32)[:, None]
    doc_lengths = jnp.where(row_index == 0, shortest, doc_lengths).astype(jnp.int32)
    offset = jnp.where(row_index == 0, shortest - 1, offset).astype(jnp.int32)
    ends = jnp.cumsum(doc_lengths, axis=1) - offset
    places = jnp.arange(L, dtype=jnp.int32)
    passed = (ends[:, None, :] <= places[None, :, None]).astype(jnp.int32)
    return jnp.sum(passed, axis=-1).astype(jnp.int32)


def with_spikes(values, stream_key, source, target, blocks, factor):
    def block_of(position):
        return (jnp.arange(values.shape[position]) // (values.shape[position] // blocks)).reshape((-1,) + (1,) * (values.ndim - 1 - position))

    one_side = jax.random.permutation(stream_key, blocks)[block_of(target)]
    other_side = (block_of(target) + blocks // 2) % blocks
    return jnp.where((block_of(source) == one_side) | (block_of(source) == other_side), factor * values, values)


def shard_levels(rng, shape, cuts, least, largest):
    level, own = 1.0, jax.random.fold_in(rng, 6)
    for axis_at, blocks in cuts:
        draws = jnp.exp(jax.random.uniform(jax.random.fold_in(own, axis_at), (blocks,), jnp.float32, least / len(cuts), largest / len(cuts)))
        level = level * jnp.repeat(draws, shape[axis_at] // blocks).reshape([-1 if axis == axis_at else 1 for axis in range(len(shape))])
    return level


def noise(key, shape, scale, limit, split=(), kind=jnp.bfloat16):
    values = jax.random.normal(key, shape, jnp.float32) * scale
    if len(split) > 0:
        values = shard_levels(key, shape, split, -0.22, 0.18) * values
    return jnp.clip(values, min=-limit, max=limit).astype(kind)


def gaussian_with(rng, dims, width, bound, pieces, heavy, kind=jnp.bfloat16):
    drawn = width * jax.random.normal(rng, dims, jnp.float32)
    if pieces:
        drawn = drawn * shard_levels(rng, dims, pieces, -0.22, 0.18)
    return jnp.clip(with_spikes(drawn, jax.random.fold_in(rng, 3), *heavy), -bound, bound).astype(kind)


def setup_inputs(seed: int = 0) -> dict:
    arg_keys = jax.random.split(jax.random.key(seed), 9)
    hidden_in = noise(arg_keys[0], (ROWS, L, D), 1.0, 6.0, ((0, 8), (1, 4)))
    cotangent = gaussian_with(arg_keys[1], (ROWS, L, D), 1.0, 6.0, ((0, 8), (1, 4)), (0, 2, 8, 2.0))
    segment_ids = draw_segment_ids(jax.random.fold_in(arg_keys[8], 71), 0)
    w_qkv = noise(arg_keys[3], (3, D, D), D ** -0.5, 0.21875, ((1, 8), (2, 4)))
    w_out = noise(arg_keys[4], (D, D), (D // 32) ** -0.5, 1.25, ((0, 4), (1, 8)))
    w_in = noise(arg_keys[5], (2, D, FF), D ** -0.5, 0.21875, ((1, 8), (2, 4)))
    w_down = noise(arg_keys[6], (FF, D), FF ** -0.5, 0.1875, ((0, 4), (1, 8)))
    norm_gains = jnp.clip(1.0 + 0.18 * jax.random.normal(arg_keys[7], (2, D), jnp.float32), 0.099609375, 1.8984375).astype(jnp.bfloat16)
    return dict(hidden_in=hidden_in, cotangent=cotangent, segment_ids=segment_ids, w_qkv=w_qkv, w_out=w_out, w_in=w_in, w_down=w_down, norm_gains=norm_gains)


EPS = 1e-05
THETA = 160000.0
HIGH = lax.Precision.HIGHEST

@jax.custom_vjp
def low(v):
    return lax.optimization_barrier(v.astype(jnp.bfloat16)).astype(jnp.float32)

@jax.custom_vjp
def low_back(v):
    return v

def low_keep(v):
    return (low(v), None)

def low_pass(kept, grad):
    return (grad,)

def back_keep(v):
    return (v, None)

def back_low(kept, grad):
    return (low(grad),)
low.defvjp(low_keep, low_pass)
low_back.defvjp(back_keep, back_low)

def layer_norm(value, gain):
    centred = value - lax.optimization_barrier(jnp.mean(value, axis=-1, keepdims=True))
    variance = lax.optimization_barrier(jnp.mean(centred * centred, axis=-1, keepdims=True))
    return centred * lax.rsqrt(variance + EPS) * gain

def positions_of(segments):
    index = lax.broadcasted_iota(jnp.int32, segments.shape, 1)
    change = jnp.concatenate([jnp.ones_like(segments[:, :1]), (segments[:, 1:] != segments[:, :-1]).astype(jnp.int32)], axis=1)
    first = lax.cummax(jnp.where(change > 0, index, 0), axis=1)
    return index - first

def rope_tables(positions, head_size):
    half = head_size // 2
    frequency = THETA ** (-2.0 * jnp.arange(half, dtype=jnp.float32) / head_size)
    angle = positions.astype(jnp.float32)[..., None] * frequency
    cosine = jnp.concatenate([jnp.cos(angle), jnp.cos(angle)], axis=-1)[..., None, :]
    sine = jnp.concatenate([jnp.sin(angle), jnp.sin(angle)], axis=-1)[..., None, :]
    return (cosine, sine)

def rotate(value, cosine, sine):
    half = value.shape[-1] // 2
    turned = jnp.concatenate([-value[..., half:], value[..., :half]], axis=-1)
    return value * cosine + turned * sine

def forward(hidden_row, w_qkv, w_out, w_in, w_down, gains, segment, cosine, sine):
    length = hidden_row.shape[0]
    norm_one = low(layer_norm(hidden_row, gains[0]))
    raw = jnp.einsum('ld,cde->lce', norm_one, w_qkv, precision=HIGH)
    query = low(rotate(low_back(raw[:, 0].reshape(length, H, HD)), cosine, sine))
    keys = low(rotate(low_back(raw[:, 1].reshape(length, H, HD)), cosine, sine))
    values = low(low_back(raw[:, 2].reshape(length, H, HD)))
    scores = low_back(jnp.einsum('qhd,khd->hqk', query, keys, precision=HIGH) * (1.0 / math.sqrt(HD)))
    allowed = (segment[:, None] == segment[None, :])[None]
    scores = jnp.where(allowed, scores, -1e+30)
    top = lax.optimization_barrier(jnp.max(scores, axis=-1, keepdims=True))
    expo = jnp.exp(scores - top)
    probs = low(expo / lax.optimization_barrier(jnp.sum(expo, axis=-1, keepdims=True)))
    mixed = jnp.einsum('hqk,khd->qhd', probs, values, precision=HIGH).reshape(length, H * HD)
    mixed = low_back(low(mixed))
    residual = hidden_row + low_back(jnp.dot(mixed, w_out, precision=HIGH))
    norm_two = low(layer_norm(residual, gains[1]))
    gate_up = low_back(jnp.einsum('ld,cdf->lcf', norm_two, w_in, precision=HIGH))
    product = low(jax.nn.gelu(gate_up[:, 0], approximate=False) * gate_up[:, 1])
    return residual + low_back(jnp.dot(product, w_down, precision=HIGH))

def reference(hidden_in, cotangent, segment_ids, w_qkv, w_out, w_in, w_down, norm_gains):
    weights = tuple((a.astype(jnp.float32) for a in (w_qkv, w_out, w_in, w_down, norm_gains)))
    positions = positions_of(segment_ids)
    cosine, sine = rope_tables(positions, HD)

    def step(totals, item):
        hidden_row, cot_row, seg_row, cos_row, sin_row = item

        def run(h_in, a_w, b_w, c_w, d_w, e_w):
            return forward(h_in, a_w, b_w, c_w, d_w, e_w, seg_row, cos_row, sin_row)
        out_row, back = jax.vjp(run, hidden_row.astype(jnp.float32), *weights)
        grads = back(cot_row.astype(jnp.float32))
        summed = tuple((t + g for t, g in zip(totals, grads[1:])))
        return (summed, (out_row.astype(jnp.bfloat16), grads[0].astype(jnp.bfloat16)))
    zeros = tuple((jnp.zeros(w.shape, jnp.float32) for w in weights))
    totals, (outputs, grad_rows) = lax.scan(step, zeros, (hidden_in, cotangent, segment_ids, cosine, sine))
    return (outputs, grad_rows, totals[0], totals[1], totals[2], totals[3], totals[4])
```

```python
import math

import jax
import jax.numpy as jnp
from jax import lax
from jax.sharding import PartitionSpec as P

HD = 64


EPS = 1e-05
THETA = 160000.0


def layer_norm(value, gain):
    centred = value - jnp.mean(value, axis=-1, keepdims=True)
    variance = jnp.mean(centred * centred, axis=-1, keepdims=True)
    return centred * lax.rsqrt(variance + EPS) * gain


def geglu(gate_up):
    return jax.nn.gelu(gate_up[..., 0, :], approximate=False) * gate_up[..., 1, :]


def positions_of(segments):
    index = lax.broadcasted_iota(jnp.int32, segments.shape, 1)
    change = jnp.concatenate(
        [jnp.ones_like(segments[:, :1]), (segments[:, 1:] != segments[:, :-1]).astype(jnp.int32)],
        axis=1,
    )
    first = lax.cummax(jnp.where(change > 0, index, 0), axis=1)
    return index - first


def rope_tables(positions, head_size):
    half = head_size // 2
    frequency = THETA ** (-2.0 * jnp.arange(half, dtype=jnp.float32) / head_size)
    angle = positions.astype(jnp.float32)[..., None] * frequency
    cosine = jnp.concatenate([jnp.cos(angle), jnp.cos(angle)], axis=-1)[..., None, :]
    sine = jnp.concatenate([jnp.sin(angle), jnp.sin(angle)], axis=-1)[..., None, :]
    return (cosine, sine)


def rotate(value, cosine, sine):
    half = value.shape[-1] // 2
    turned = jnp.concatenate([-value[..., half:], value[..., :half]], axis=-1)
    return value * cosine + turned * sine


def rotate_back(grad, cosine, sine):
    half = grad.shape[-1] // 2
    scaled = grad * sine
    turned = jnp.concatenate([scaled[..., half:], -scaled[..., :half]], axis=-1)
    return grad * cosine + turned


def attend(item):
    query, keys, values, allowed = item
    scale = 1.0 / math.sqrt(query.shape[-1])
    scores = jnp.einsum("qhd,khd->hqk", query, keys, preferred_element_type=jnp.float32) * scale
    scores = jnp.where(allowed[None], scores, -1e30)
    top = jnp.max(scores, axis=-1, keepdims=True)
    expo = jnp.exp(scores - top)
    total = jnp.sum(expo, axis=-1, keepdims=True)
    probs = expo / total
    mixed = jnp.einsum(
        "hqk,khd->qhd", probs.astype(jnp.bfloat16), values, preferred_element_type=jnp.float32
    )
    return (mixed.astype(jnp.bfloat16), (top + jnp.log(total))[..., 0])


def attend_back(item):
    query, keys, values, allowed, logsum, grad_mixed = item
    scale = 1.0 / math.sqrt(query.shape[-1])
    scores = jnp.einsum("qhd,khd->hqk", query, keys, preferred_element_type=jnp.float32) * scale
    scores = jnp.where(allowed[None], scores, -1e30)
    probs = jnp.exp(scores - logsum[..., None])
    grad_values = jnp.einsum(
        "hqk,qhd->khd", probs.astype(jnp.bfloat16), grad_mixed, preferred_element_type=jnp.float32
    )
    grad_probs = jnp.einsum("qhd,khd->hqk", grad_mixed, values, preferred_element_type=jnp.float32)
    grad_scores = probs * (grad_probs - jnp.sum(probs * grad_probs, axis=-1, keepdims=True))
    grad_scaled = (grad_scores * scale).astype(jnp.bfloat16)
    grad_query = jnp.einsum("hqk,khd->qhd", grad_scaled, keys, preferred_element_type=jnp.float32)
    grad_keys = jnp.einsum("hqk,qhd->khd", grad_scaled, query, preferred_element_type=jnp.float32)
    return (grad_query, grad_keys, grad_values)


def mm(spec, a, b):
    return jnp.einsum(spec, a, b, preferred_element_type=jnp.float32)


def shards(hidden_in, cotangent, segment_ids, w_qkv, w_out, w_in, w_down, norm_gains):
    ndp, nt = lax.axis_size("dp"), lax.axis_size("tensor")
    bf, f32 = jnp.bfloat16, jnp.float32
    core = lax.axis_index("dp") % 2
    place = lax.axis_index("tensor")
    rows, local_len, width = hidden_in.shape
    half = local_len // 2
    tokens = nt * half

    def swap(v):
        return lax.ppermute(v, "dp", [(i, i ^ 1) for i in range(ndp)])

    def in_order(mine, other, axis):
        return jnp.where(
            core == 0,
            jnp.concatenate([mine, other], axis=axis),
            jnp.concatenate([other, mine], axis=axis),
        )

    def pick(v, index, axis):
        return lax.dynamic_index_in_dim(v, index, axis, keepdims=False)

    def enter(v):
        v = v.reshape(rows, 2, half, width)
        v = in_order(pick(v, core, 1), swap(pick(v, 1 - core, 1)), 0)
        return lax.all_to_all(v, "tensor", 0, 0, tiled=True).reshape(tokens, width)

    def leave(v):
        v = lax.all_to_all(v.reshape(nt, half, width), "tensor", 0, 0, tiled=True)
        v = v.reshape(2, rows, 1, half, width)
        v = in_order(pick(v, core, 0), swap(pick(v, 1 - core, 0)), 1)
        return v.reshape(rows, local_len, width)

    def gather(v):
        return lax.all_gather(lax.all_gather(v, "tensor"), "dp")

    def scatter(v):
        v = lax.psum_scatter(v.astype(bf), "dp", scatter_dimension=0)
        return lax.psum_scatter(v, "tensor", scatter_dimension=0).astype(f32)

    dl, el, fl = w_qkv.shape[1], w_qkv.shape[2], w_in.shape[2]
    ff = fl * nt

    def whole(v, n, cols):
        v = v.reshape(ndp, nt, dl, n, cols)
        return jnp.transpose(v, (3, 0, 2, 1, 4)).reshape(n, ndp * dl, nt * cols)

    def parted(v, n, cols):
        v = v.reshape(n, ndp, dl, nt, cols)
        return jnp.transpose(v, (1, 3, 2, 0, 4)).reshape(ndp, nt, dl, n * cols)

    def flat(v):
        return jnp.transpose(v, (1, 0, 2)).reshape(dl, -1)

    first = gather(jnp.concatenate([flat(w_qkv), w_out.T], axis=1))
    qkv_all = whole(first[..., : 3 * el], 3, el)
    out_t = whole(first[..., 3 * el :], 1, el)[0]
    second = gather(jnp.concatenate([flat(w_in), w_down.T], axis=1))
    in_all = whole(second[..., : 2 * fl], 2, fl)
    down_t = whole(second[..., 2 * fl :], 1, fl)[0]
    gains_all = lax.all_gather(norm_gains, "dp", axis=1, tiled=True)
    gain_one = gains_all[0].astype(f32)
    gain_two = gains_all[1].astype(f32)

    segments = in_order(segment_ids, swap(segment_ids), 0)
    spots = positions_of(segments)
    row_seg = pick(segments, place, 0).reshape(nt, 2, half)
    row_pos = pick(spots, place, 0).reshape(nt, 2, half)
    seg_q = pick(row_seg, core, 1).reshape(tokens)
    seg_k = jnp.concatenate([seg_q, pick(row_seg, 1 - core, 1).reshape(tokens)])
    cosine, sine = rope_tables(pick(row_pos, core, 1).reshape(tokens), HD)
    allowed = seg_q[:, None] == seg_k[None, :]

    hidden_f = enter(hidden_in).astype(f32)
    cot = enter(cotangent)
    normed_one, norm_one_back = jax.vjp(layer_norm, hidden_f, gain_one)
    norm_one_low = normed_one.astype(bf)
    heads = width // HD
    groups = heads // 3
    projected = [mm("ld,de->le", norm_one_low, qkv_all[c]).reshape(tokens, heads, HD) for c in range(3)]
    query = rotate(projected[0], cosine, sine).astype(bf)
    keys = rotate(projected[1], cosine, sine).astype(bf)
    values = projected[2].astype(bf)
    pair = jnp.stack([keys, values])
    pair = jnp.concatenate([pair, swap(pair)], axis=1)

    def grouped(v):
        return jnp.moveaxis(v.reshape(v.shape[0], groups, 3, HD), 1, 0)

    def ungrouped(v):
        return jnp.moveaxis(v, 0, 1).reshape(v.shape[1], width)

    q_g, k_g, v_g = grouped(query), grouped(pair[0]), grouped(pair[1])
    mixed_g, logsum = lax.map(lambda it: attend((*it, allowed)), (q_g, k_g, v_g))
    mixed = ungrouped(mixed_g)
    residual = hidden_f + mm("lk,dk->ld", mixed, out_t)
    normed_two, norm_two_back = jax.vjp(layer_norm, residual, gain_two)
    norm_two_low = normed_two.astype(bf)
    gate_up = jnp.stack([mm("ld,df->lf", norm_two_low, in_all[c]) for c in range(2)], axis=-2)
    product_f, product_back = jax.vjp(geglu, gate_up)
    product = product_f.astype(bf)
    layer_out = leave((residual + mm("lf,df->ld", product, down_t)).astype(bf))

    grad_down_t = mm("ld,lf->df", cot, product)
    grad_gate_up = product_back(mm("ld,df->lf", cot, down_t))[0].astype(bf)
    g_gate, g_up = grad_gate_up[:, 0], grad_gate_up[:, 1]
    grad_in_full = jnp.stack([mm("ld,lf->df", norm_two_low, g).astype(bf) for g in (g_gate, g_up)])
    second_grad = scatter(
        jnp.concatenate([parted(grad_in_full, 2, fl), parted(grad_down_t.astype(bf), 1, fl)], axis=-1)
    )
    grad_norm_two = mm("lf,df->ld", g_gate, in_all[0]) + mm("lf,df->ld", g_up, in_all[1])
    grad_from_two, gain_two_part = norm_two_back(grad_norm_two)
    grad_residual = cot.astype(f32) + grad_from_two
    residual_low = grad_residual.astype(bf)
    grad_out_t = mm("ld,lk->dk", residual_low, mixed).astype(bf)
    grad_mixed = mm("ld,dk->lk", residual_low, out_t).astype(bf).reshape(tokens, heads, HD)
    gq, gk, gv = lax.map(
        lambda it: attend_back((it[0], it[1], it[2], allowed, it[3], it[4])),
        (q_g, k_g, v_g, logsum, grouped(grad_mixed)),
    )
    gq, gk, gv = ungrouped(gq), ungrouped(gk), ungrouped(gv)
    away = swap(jnp.stack([gk[tokens:], gv[tokens:]]).astype(bf)).astype(f32)
    shape = (tokens, heads, HD)
    grad_query = rotate_back(gq.reshape(shape), cosine, sine)
    grad_keys = rotate_back((gk[:tokens] + away[0]).reshape(shape), cosine, sine)
    raws = [
        grad_query.astype(bf).reshape(tokens, width),
        grad_keys.astype(bf).reshape(tokens, width),
        (gv[:tokens] + away[1]).astype(bf),
    ]
    grad_qkv_full = jnp.stack([mm("ld,le->de", norm_one_low, r).astype(bf) for r in raws])
    first_grad = scatter(
        jnp.concatenate([parted(grad_qkv_full, 3, el), parted(grad_out_t, 1, el)], axis=-1)
    )
    grad_norm_one = sum(mm("le,de->ld", raws[c], qkv_all[c]) for c in range(3))
    grad_from_one, gain_one_part = norm_one_back(grad_norm_one)
    grad_input = leave((grad_residual + grad_from_one).astype(bf))
    gains_part = jnp.stack([gain_one_part, gain_two_part], axis=0)
    grad_gains = lax.psum_scatter(gains_part, "dp", scatter_dimension=1, tiled=True)
    grad_gains = lax.psum(grad_gains, "tensor")

    def stacked(v, n, cols):
        return jnp.transpose(v.reshape(dl, n, cols), (1, 0, 2))

    grad_qkv = stacked(first_grad[:, : 3 * el], 3, el)
    grad_out = first_grad[:, 3 * el :].T
    grad_in = stacked(second_grad[:, : 2 * fl], 2, fl)
    grad_down = second_grad[:, 2 * fl :].T
    return (layer_out, grad_input, grad_qkv, grad_out, grad_in, grad_down, grad_gains)


def solution(mesh):
    placed = (
        P("dp", "tensor", None),
        P("dp", "tensor", None),
        P("dp", None),
        P(None, "dp", "tensor"),
        P("tensor", "dp"),
        P(None, "dp", "tensor"),
        P("tensor", "dp"),
        P(None, "dp"),
    )
    return jax.shard_map(
        shards,
        mesh=mesh,
        in_specs=placed,
        out_specs=(
            P("dp", "tensor", None),
            P("dp", "tensor", None),
            P(None, "dp", "tensor"),
            P("tensor", "dp"),
            P(None, "dp", "tensor"),
            P("tensor", "dp"),
            P(None, "dp"),
        ),
        check_vma=False,
    )
```

```python
import math

import jax
import jax.numpy as jnp
from jax import lax
from jax.experimental import pallas as pl
from jax.experimental.pallas import tpu as pltpu
from jax.sharding import PartitionSpec as P

HD = 64


EPS = 1e-05
THETA = 160000.0


def layer_norm(value, gain):
    centred = value - jnp.mean(value, axis=-1, keepdims=True)
    variance = jnp.mean(centred * centred, axis=-1, keepdims=True)
    return centred * lax.rsqrt(variance + EPS) * gain


def positions_of(segments):
    index = lax.broadcasted_iota(jnp.int32, segments.shape, 1)
    change = jnp.concatenate(
        [jnp.ones_like(segments[:, :1]), (segments[:, 1:] != segments[:, :-1]).astype(jnp.int32)],
        axis=1,
    )
    first = lax.cummax(jnp.where(change > 0, index, 0), axis=1)
    return index - first


def rope_tables(positions, head_size):
    half = head_size // 2
    frequency = THETA ** (-2.0 * jnp.arange(half, dtype=jnp.float32) / head_size)
    angle = positions.astype(jnp.float32)[..., None] * frequency
    cosine = jnp.concatenate([jnp.cos(angle), jnp.cos(angle)], axis=-1)[..., None, :]
    sine = jnp.concatenate([jnp.sin(angle), jnp.sin(angle)], axis=-1)[..., None, :]
    return (cosine, sine)


def turn(value):
    half = HD // 2
    ahead = jnp.concatenate([value[..., half:], value[..., :half]], axis=-1)
    behind = jnp.concatenate([value[..., -half:], value[..., :-half]], axis=-1)
    lane = lax.broadcasted_iota(jnp.int32, value.shape, value.ndim - 1)
    return jnp.where(lane % HD < half, -ahead, behind)


def rotate(value, cosine, sine):
    return value * cosine + turn(value) * sine


def rotate_back(grad, cosine, sine):
    return grad * cosine - turn(grad * sine)


def dot(a, b, dims):
    return lax.dot_general(a, b, (dims, ((), ())), preferred_element_type=jnp.float32)


def probs_of(query, keys, allowed):
    scores = dot(keys, query, ((1,), (1,))) * (1.0 / math.sqrt(HD))
    scores = jnp.where(allowed, scores, -1e30)
    expo = jnp.exp(scores - jnp.max(scores, axis=0, keepdims=True))
    return expo * (1.0 / jnp.sum(expo, axis=0, keepdims=True))


def attend_kernel(q_ref, k_ref, v_ref, sq_ref, sk_ref, o_ref):
    allowed = sk_ref[...] == sq_ref[...]
    for h in range(q_ref.shape[2] // HD):
        at = slice(h * HD, (h + 1) * HD)
        probs = probs_of(q_ref[0, :, at], k_ref[0, :, at], allowed)
        mixed = dot(probs.astype(jnp.bfloat16), v_ref[0, :, at], ((0,), (0,)))
        o_ref[0, :, at] = mixed.astype(jnp.bfloat16)


def attend_back_kernel(q_ref, k_ref, v_ref, g_ref, sq_ref, sk_ref, gq_ref, gk_ref, gv_ref):
    allowed = sk_ref[...] == sq_ref[...]
    for h in range(q_ref.shape[2] // HD):
        at = slice(h * HD, (h + 1) * HD)
        query, keys, values, grad = q_ref[0, :, at], k_ref[0, :, at], v_ref[0, :, at], g_ref[0, :, at]
        probs = probs_of(query, keys, allowed)
        gv_ref[0, :, at] = dot(probs.astype(jnp.bfloat16), grad, ((1,), (0,)))
        grad_probs = dot(values, grad, ((1,), (1,)))
        inner = jnp.sum(probs * grad_probs, axis=0, keepdims=True)
        scaled = (probs * (grad_probs - inner) * (1.0 / math.sqrt(HD))).astype(jnp.bfloat16)
        gq_ref[0, :, at] = dot(scaled, keys, ((0,), (0,)))
        gk_ref[0, :, at] = dot(scaled, query, ((1,), (0,)))


def attention(kernel, arrays, seg_q, seg_k, lengths, dtype):
    groups, _, lanes = arrays[0].shape
    block = lambda n: pl.BlockSpec((1, n, lanes), lambda i: (i, 0, 0))
    fixed = lambda shape: pl.BlockSpec(shape, lambda i: (0, 0))
    sq, sk = seg_q[None, :], seg_k[:, None]
    return pl.pallas_call(
        kernel,
        grid=(groups,),
        in_specs=[block(v.shape[1]) for v in arrays] + [fixed(sq.shape), fixed(sk.shape)],
        out_specs=[block(n) for n in lengths],
        out_shape=[jax.ShapeDtypeStruct((groups, n, lanes), dtype) for n in lengths],
        compiler_params=pltpu.CompilerParams(vmem_limit_bytes=48 * 1024 * 1024),
    )(*arrays, sq, sk)


def mm(spec, a, b):
    return jnp.einsum(spec, a, b, preferred_element_type=jnp.float32)


def shards(hidden_in, cotangent, segment_ids, w_qkv, w_out, w_in, w_down, norm_gains):
    ndp, nt = lax.axis_size("dp"), lax.axis_size("tensor")
    bf, f32 = jnp.bfloat16, jnp.float32
    core = lax.axis_index("dp") % 2
    place = lax.axis_index("tensor")
    rows, local_len, width = hidden_in.shape
    half = local_len // 2
    tokens = nt * half

    def swap(v):
        return lax.ppermute(v, "dp", [(i, i ^ 1) for i in range(ndp)])

    def in_order(mine, other, axis):
        return jnp.where(
            core == 0,
            jnp.concatenate([mine, other], axis=axis),
            jnp.concatenate([other, mine], axis=axis),
        )

    def pick(v, index, axis):
        return lax.dynamic_index_in_dim(v, index, axis, keepdims=False)

    def enter(v):
        v = v.reshape(rows, 2, half, width)
        v = in_order(pick(v, core, 1), swap(pick(v, 1 - core, 1)), 0)
        return lax.all_to_all(v, "tensor", 0, 0, tiled=True).reshape(tokens, width)

    def leave(v):
        v = lax.all_to_all(v.reshape(nt, half, width), "tensor", 0, 0, tiled=True)
        v = v.reshape(2, rows, 1, half, width)
        v = in_order(pick(v, core, 0), swap(pick(v, 1 - core, 0)), 1)
        return v.reshape(rows, local_len, width)

    def gather(v):
        v = lax.all_gather(lax.all_gather(v, "tensor"), "dp")
        return jnp.swapaxes(v, 0, 1).reshape(nt, width, v.shape[-1])

    def scatter(v):
        v = jnp.swapaxes(v.reshape(nt, ndp, width // ndp, v.shape[-1]), 0, 1)
        v = v.reshape(nt * width, v.shape[-1])
        v = lax.psum_scatter(v, "dp", scatter_dimension=0, tiled=True)
        return lax.psum_scatter(v, "tensor", scatter_dimension=0, tiled=True).astype(f32)

    dl, el, fl = w_qkv.shape[1], w_qkv.shape[2], w_in.shape[2]

    def flat(v):
        return jnp.transpose(v, (1, 0, 2)).reshape(dl, -1)

    qkv_all = gather(flat(w_qkv))
    second = gather(jnp.concatenate([flat(w_in), w_out.T, w_down.T], axis=1))
    two, three = 2 * fl, 2 * fl + el
    in_all, out_t, down_t = second[..., :two], second[..., two:three], second[..., three:]
    gains_all = lax.all_gather(norm_gains, "dp", axis=1, tiled=True)
    gain_one = gains_all[0].astype(f32)
    gain_two = gains_all[1].astype(f32)

    segments = in_order(segment_ids, swap(segment_ids), 0)
    spots = positions_of(segments)
    row_seg = pick(segments, place, 0).reshape(nt, 2, half)
    row_pos = pick(spots, place, 0).reshape(nt, 2, half)
    seg_q = pick(row_seg, core, 1).reshape(tokens)
    seg_k = jnp.concatenate([seg_q, pick(row_seg, 1 - core, 1).reshape(tokens)])
    cosine, sine = rope_tables(pick(row_pos, core, 1).reshape(tokens), HD)
    cosine = jnp.tile(cosine[:, 0], (1, el // HD))
    sine = jnp.tile(sine[:, 0], (1, el // HD))

    hidden_f = enter(hidden_in).astype(f32)
    cot = enter(cotangent)
    normed_one, norm_one_back = jax.vjp(layer_norm, hidden_f, gain_one)
    norm_one_low = normed_one.astype(bf)
    projected = mm("ld,tde->tle", norm_one_low, qkv_all)
    query = rotate(projected[..., :el], cosine, sine).astype(bf)
    keys = rotate(projected[..., el : 2 * el], cosine, sine).astype(bf)
    values = projected[..., 2 * el :].astype(bf)
    pair = jnp.stack([keys, values])
    pair = jnp.concatenate([pair, swap(pair)], axis=2)
    keys, values = pair[0], pair[1]
    mixed = attention(attend_kernel, (query, keys, values), seg_q, seg_k, (tokens,), bf)[0]
    residual = hidden_f + mm("tlk,tdk->ld", mixed, out_t)
    normed_two, norm_two_back = jax.vjp(layer_norm, residual, gain_two)
    norm_two_low = normed_two.astype(bf)
    gate_up = mm("ld,tde->tle", norm_two_low, in_all)
    geglu = lambda gate, up: jax.nn.gelu(gate, approximate=False) * up
    product_f, product_back = jax.vjp(geglu, gate_up[..., :fl], gate_up[..., fl:])
    product = product_f.astype(bf)
    layer_out = leave((residual + mm("tlf,tdf->ld", product, down_t)).astype(bf))

    grad_down_t = mm("ld,tlf->tdf", cot, product).astype(bf)
    grad_gate_up = jnp.concatenate(
        [v.astype(bf) for v in product_back(mm("ld,tdf->tlf", cot, down_t))], axis=-1
    )
    grad_in_full = mm("ld,tle->tde", norm_two_low, grad_gate_up).astype(bf)
    grad_norm_two = mm("tle,tde->ld", grad_gate_up, in_all)
    grad_from_two, gain_two_part = norm_two_back(grad_norm_two)
    grad_residual = cot.astype(f32) + grad_from_two
    residual_low = grad_residual.astype(bf)
    grad_out_t = mm("ld,tlk->tdk", residual_low, mixed).astype(bf)
    second_grad = scatter(jnp.concatenate([grad_in_full, grad_out_t, grad_down_t], axis=-1))
    grad_mixed = mm("ld,tdk->tlk", residual_low, out_t).astype(bf)
    gq, gk, gv = attention(
        attend_back_kernel,
        (query, keys, values, grad_mixed),
        seg_q,
        seg_k,
        (tokens, 2 * tokens, 2 * tokens),
        f32,
    )
    away = swap(jnp.stack([gk[:, tokens:], gv[:, tokens:]]).astype(bf)).astype(f32)
    grad_raw = jnp.concatenate(
        [
            rotate_back(gq, cosine, sine).astype(bf),
            rotate_back(gk[:, :tokens] + away[0], cosine, sine).astype(bf),
            (gv[:, :tokens] + away[1]).astype(bf),
        ],
        axis=-1,
    )
    first_grad = scatter(mm("ld,tle->tde", norm_one_low, grad_raw).astype(bf))
    grad_norm_one = mm("tle,tde->ld", grad_raw, qkv_all)
    grad_from_one, gain_one_part = norm_one_back(grad_norm_one)
    grad_input = leave((grad_residual + grad_from_one).astype(bf))
    gains_part = jnp.stack([gain_one_part, gain_two_part], axis=0)
    gains_sum = lax.psum(gains_part, ("dp", "tensor"))
    grad_gains = lax.dynamic_slice_in_dim(gains_sum, lax.axis_index("dp") * dl, dl, 1)

    def stacked(v, n, cols):
        return jnp.transpose(v.reshape(dl, n, cols), (1, 0, 2))

    grad_qkv = stacked(first_grad, 3, el)
    grad_out = second_grad[:, two:three].T
    grad_in = stacked(second_grad[:, :two], 2, fl)
    grad_down = second_grad[:, three:].T
    return (layer_out, grad_input, grad_qkv, grad_out, grad_in, grad_down, grad_gains)


def solution(mesh):
    placed = (
        P("dp", "tensor", None),
        P("dp", "tensor", None),
        P("dp", None),
        P(None, "dp", "tensor"),
        P("tensor", "dp"),
        P(None, "dp", "tensor"),
        P("tensor", "dp"),
        P(None, "dp"),
    )
    return jax.shard_map(
        shards,
        mesh=mesh,
        in_specs=placed,
        out_specs=(
            P("dp", "tensor", None),
            P("dp", "tensor", None),
            P(None, "dp", "tensor"),
            P("tensor", "dp"),
            P(None, "dp", "tensor"),
            P("tensor", "dp"),
            P(None, "dp"),
        ),
        check_vma=False,
    )
```
